32 devices in a mesh: tm: 4 (over y, core), dom: 8 (over z, x).
Axes of the slice: x: 2, y: 2, z: 4, core: 2. Of those that a mesh axis runs over, the one named last changes fastest.
Arguments:
- particles: float32 [4, 64, 4096], P('tm', None, 'dom'), may hold values from -12 to 12, as said below
- noise: float32 [4, 64, 4096], P('tm', None, 'dom'), may hold values from -6 to 6
Outputs:
- advanced: float32 [4, 64, 4096], P('tm', None, 'dom')
The draws below stay inside these ranges and needn't reach their ends.
Inputs may be any that keep to these rules, and one draw needn't show every extreme that they name: `particles`: positions of cells in principal components, each time point about a shifted centre.
All inputs are finite; a program needn't handle non-finite values.
Results may differ from the reference program's by a relative error of at most 0.012.
The reference program's roundings to bfloat16 on the way count: a program that leaves them out, or rounds other values in their place, can miss the bound.
Values may be sent and summed in bfloat16 or wider, within the bound.
A program may use at most 64 MiB of HBM per device.

```python
import math
import jax
import jax.numpy as jnp
from jax import lax

DIM = 64
SWEEPS = 2
NPART = 4096
TIMES = 4


def draw_particles(key, part):
    shape = (TIMES, DIM, NPART)
    centres = 0.3 * jnp.arange(TIMES, dtype=jnp.float32)[:, None, None]
    base = jnp.clip(jax.random.normal(jax.random.fold_in(key, 3), shape, jnp.float32), -6.0, 6.0)
    return base + centres


def block_levels(rng, shape, cuts, smallest, high):
    gain, own = 1.0, jax.random.fold_in(rng, 6)
    for axis_at, blocks in cuts:
        heights = jnp.exp(jax.random.uniform(jax.random.fold_in(own, axis_at), (blocks,), jnp.float32, smallest / len(cuts), high / len(cuts)))
        gain = gain * jnp.repeat(heights, shape[axis_at] // blocks).reshape([-1 if axis == axis_at else 1 for axis in range(len(shape))])
    return gain


def centred(own_key, shape, deviation, reach, shards=(), kind=jnp.bfloat16):
    loudness = block_levels(own_key, shape, shards, -0.22, 0.18) if shards else 1.0
    values = jax.random.normal(own_key, shape, jnp.float32) * deviation * loudness
    return jnp.minimum(jnp.maximum(values, -reach), reach).astype(kind)


def setup_inputs(seed: int = 0) -> dict:
    arg_keys = jax.random.split(jax.random.key(seed), 3)
    particles = draw_particles(jax.random.fold_in(arg_keys[2], 71), 0)
    noise = centred(arg_keys[1], (TIMES, DIM, NPART), 1.0, 6.0, ((0, 4), (2, 8)), jnp.float32)
    return {"particles": particles, "noise": noise}


EPS = 4.0
STEP = 0.5
TEMP = 0.05

def row_blocks(sources):
    row_count = sources.shape[1]
    row_width = math.gcd(row_count, 512)
    return sources.reshape(DIM, row_count // row_width, row_width).transpose(1, 0, 2)

def scores_of(sources, targets, potential):
    products = lax.dot_general(sources, targets, (((0,), (0,)), ((), ())), preferred_element_type=jnp.float32)
    return (products + potential[None, :]) / EPS

def update(sources, targets, potential):
    col_count = targets.shape[1]

    def per_block(blocks):
        scores = scores_of(blocks, targets, potential)
        highest = lax.optimization_barrier(jnp.max(scores, axis=1, keepdims=True))
        totals = lax.optimization_barrier(jnp.sum(jnp.exp(scores - highest), axis=1))
        return -EPS * (highest[:, 0] + jnp.log(totals)) + EPS * math.log(col_count)
    return lax.map(per_block, row_blocks(sources)).reshape(sources.shape[1])

def barycentre(sources, targets, potential):

    def per_block(blocks):
        scores = scores_of(blocks, targets, potential)
        highest = lax.optimization_barrier(jnp.max(scores, axis=1, keepdims=True))
        shifted = jnp.exp(scores - highest)
        totals = lax.optimization_barrier(jnp.sum(shifted, axis=1, keepdims=True))
        weights = (shifted / totals).astype(jnp.bfloat16)
        return lax.dot_general(targets, weights, (((1,), (1,)), ((), ())), preferred_element_type=jnp.float32)
    result = lax.map(per_block, row_blocks(sources))
    return result.transpose(1, 0, 2).reshape(DIM, sources.shape[1])

def reference(particles, noise):
    rounded = particles.astype(jnp.bfloat16)
    half_square = 0.5 * lax.optimization_barrier(jnp.sum(jnp.square(rounded.astype(jnp.float32)), axis=1))
    source_pot = [None] * (TIMES - 1)
    target_pot = [-half_square[moment + 1] for moment in range(TIMES - 1)]
    for sweep_index in range(SWEEPS):
        for moment in range(TIMES - 1):
            source_pot[moment] = update(rounded[moment], rounded[moment + 1], target_pot[moment])
            target_pot[moment] = update(rounded[moment + 1], rounded[moment], source_pot[moment])
    results = []
    for moment in range(TIMES):
        pull = jnp.zeros((DIM, NPART), jnp.float32)
        if moment < TIMES - 1:
            pull = pull + (particles[moment] - barycentre(rounded[moment], rounded[moment + 1], target_pot[moment]))
        if moment > 0:
            pull = pull + (particles[moment] - barycentre(rounded[moment], rounded[moment - 1], source_pot[moment - 1]))
        results.append(particles[moment] - STEP * pull + math.sqrt(2.0 * STEP * TEMP) * noise[moment])
    return jnp.stack(results)
```

```python
import functools
import math

import jax
import jax.numpy as jnp
from jax import lax
from jax.experimental import pallas as pl
from jax.experimental.pallas import tpu as pltpu
from jax.sharding import PartitionSpec as P

SWEEPS = 2
EPS = 4.0
STEP = 0.5
TEMP = 0.05
MESH = pl.DeviceIdType.MESH
EXTRA = 16
CHUNK = 256


def crossed(me, i, n):
    total = 0
    bit = 1
    while bit < n:
        mine, its = (me // bit) % 2, (i // bit) % 2
        total = total + bit * (mine + its - 2 * mine * its)
        bit *= 2
    return total


def kernel(
    times, n, points_ref, pull_ref,
    own, nxt, prv, npot, ppot, spot, tpot, xa, ya, m_ref, l_ref, acc,
    own_s, own_r, nxt_s, nxt_r, prv_s, prv_r, npot_s, npot_r, ppot_s, ppot_r,
):
    t = lax.axis_index("tm")
    me = lax.axis_index("dom")
    dim, width = points_ref.shape
    has_next = t < times - 1
    has_prev = t > 0
    low = 2 if n > 1 else 1
    log_count = EPS * math.log(n * width)

    points = points_ref[...]
    rounded = points.astype(jnp.bfloat16)
    own[me] = rounded
    xa[pl.ds(0, dim), :] = (rounded.astype(jnp.float32) * (1.0 / EPS)).astype(jnp.bfloat16)
    rows = lax.broadcasted_iota(jnp.int32, (EXTRA, width), 0)
    xa[pl.ds(dim, EXTRA), :] = jnp.where(rows < 3, 1.0 / EPS, 0.0).astype(jnp.bfloat16)

    barrier = pltpu.get_barrier_semaphore()
    same = [i for i in range(1, n) if i % low == 0 or i == 1]
    for i in same:
        pl.semaphore_signal(barrier, inc=1, device_id=(t, crossed(me, i, n)), device_id_type=MESH)

    @pl.when(has_next)
    def _():
        for i in range(n):
            pl.semaphore_signal(barrier, inc=1, device_id=(t + 1, crossed(me, i, n)), device_id_type=MESH)

    @pl.when(has_prev)
    def _():
        for i in range(n):
            pl.semaphore_signal(barrier, inc=1, device_id=(t - 1, crossed(me, i, n)), device_id_type=MESH)

    sides = has_next.astype(jnp.int32) + has_prev.astype(jnp.int32)
    pl.semaphore_wait(barrier, len(same) + n * sides)

    def own_copy(i, block, slot):
        return pltpu.make_async_remote_copy(
            src_ref=own.at[block], dst_ref=own.at[block], send_sem=own_s.at[slot], recv_sem=own_r.at[block],
            device_id=(t, crossed(me, i, n)), device_id_type=MESH)

    def to_prev(block):
        return pltpu.make_async_remote_copy(
            src_ref=own.at[block], dst_ref=nxt.at[block], send_sem=nxt_s.at[block], recv_sem=nxt_r.at[block],
            device_id=(t - 1, me), device_id_type=MESH)

    def to_next(block):
        return pltpu.make_async_remote_copy(
            src_ref=own.at[block], dst_ref=prv.at[block], send_sem=prv_s.at[block], recv_sem=prv_r.at[block],
            device_id=(t + 1, me), device_id_type=MESH)

    for i in range(low, n, low):
        own_copy(i, me, i).start()

    def pass_on(i):
        block = crossed(me, i, n)
        if i > 0:
            own_copy(i if i % low == 0 else 1, block, 0).wait_recv()
        if i % low == 0 and low > 1:
            own_copy(1, block, i + 1).start()

        @pl.when(has_prev)
        def _():
            to_prev(block).start()

        @pl.when(has_next)
        def _():
            to_next(block).start()

    order = [0]
    for i in range(low, n, low):
        order += [i, i - low + 1] if low > 1 else [i]
    if low > 1:
        order.append(n - 1)
    for i in order:
        pass_on(i)

    def extend(block_ref, pot):
        ya[pl.ds(0, dim), :] = block_ref[...]
        high = pot.astype(jnp.bfloat16).astype(jnp.float32)
        rest = pot - high
        middle = rest.astype(jnp.bfloat16).astype(jnp.float32)
        least = rest - middle
        pieces = jnp.where(rows == 0, high, jnp.where(rows == 1, middle, jnp.where(rows == 2, least, 0.0)))
        ya[pl.ds(dim, EXTRA), :] = pieces.astype(jnp.bfloat16)

    def scores_of(start):
        return lax.dot_general(
            ya[:, pl.ds(start, CHUNK)], xa[...], (((0,), (0,)), ((), ())), preferred_element_type=jnp.float32)

    def reset():
        m_ref[...] = jnp.full_like(m_ref, -jnp.inf)
        l_ref[...] = jnp.zeros_like(l_ref)

    def log_block():
        for start in range(0, width, CHUNK):
            scores = scores_of(start)
            m_old = m_ref[...]
            m_new = jnp.maximum(m_old, jnp.max(scores, axis=0, keepdims=True))
            l_ref[...] = l_ref[...] * jnp.exp(m_old - m_new) + jnp.sum(
                jnp.exp(scores - m_new), axis=0, keepdims=True)
            m_ref[...] = m_new

    def mean_block(block_ref, total):
        for start in range(0, width, CHUNK):
            scores = scores_of(start)
            m_old = m_ref[...]
            m_new = jnp.maximum(m_old, jnp.max(scores, axis=0, keepdims=True))
            scale = jnp.exp(m_old - m_new)
            weights = jnp.exp(scores - m_new)
            l_ref[...] = l_ref[...] * scale + jnp.sum(weights, axis=0, keepdims=True)
            m_ref[...] = m_new
            total[...] = total[...] * scale + lax.dot_general(
                block_ref[:, pl.ds(start, CHUNK)], weights.astype(jnp.bfloat16), (((1,), (0,)), ((), ())),
                preferred_element_type=jnp.float32)

    def result():
        return -EPS * (m_ref[...] + jnp.log(l_ref[...])) + log_count

    def spot_copy(sweep, i):
        return pltpu.make_async_remote_copy(
            src_ref=spot.at[sweep], dst_ref=ppot.at[sweep, me], send_sem=ppot_s.at[sweep, i],
            recv_sem=ppot_r.at[sweep, me], device_id=(t + 1, crossed(me, i, n)), device_id_type=MESH)

    def tpot_copy(sweep, i):
        return pltpu.make_async_remote_copy(
            src_ref=tpot.at[sweep], dst_ref=npot.at[sweep, me], send_sem=npot_s.at[sweep, i],
            recv_sem=npot_r.at[sweep, me], device_id=(t - 1, crossed(me, i, n)), device_id_type=MESH)

    def await_ppot(sweep, block):
        pltpu.make_async_remote_copy(
            src_ref=spot.at[sweep], dst_ref=ppot.at[sweep, block], send_sem=ppot_s.at[sweep, 0],
            recv_sem=ppot_r.at[sweep, block], device_id=(t - 1, block), device_id_type=MESH).wait_recv()

    def await_npot(sweep, block):
        pltpu.make_async_remote_copy(
            src_ref=tpot.at[sweep], dst_ref=npot.at[sweep, block], send_sem=npot_s.at[sweep, 0],
            recv_sem=npot_r.at[sweep, block], device_id=(t + 1, block), device_id_type=MESH).wait_recv()

    def source_pass(sweep):
        @pl.when(has_next)
        def _():
            reset()

            @pl.loop(0, n)
            def _(i):
                block = crossed(me, i, n)
                if sweep == 0:
                    to_prev_like(block, nxt, nxt_s, nxt_r, t + 1).wait_recv()
                    extend(nxt.at[block], -0.5 * jnp.sum(
                        jnp.square(nxt[block].astype(jnp.float32)), axis=0, keepdims=True))
                else:
                    await_npot(sweep - 1, block)
                    extend(nxt.at[block], npot[sweep - 1, block])
                log_block()

            spot[sweep] = result()
            for i in reversed(range(n)):
                spot_copy(sweep, i).start()

    def to_prev_like(block, slots, sends, recvs, where):
        return pltpu.make_async_remote_copy(
            src_ref=own.at[block], dst_ref=slots.at[block], send_sem=sends.at[block], recv_sem=recvs.at[block],
            device_id=(where, me), device_id_type=MESH)

    def target_pass(sweep):
        @pl.when(has_prev)
        def _():
            reset()
            if sweep == SWEEPS - 1:
                acc[...] = jnp.zeros_like(acc)

            @pl.loop(0, n)
            def _(i):
                block = crossed(me, i, n)
                if sweep == 0:
                    to_prev_like(block, prv, prv_s, prv_r, t - 1).wait_recv()
                await_ppot(sweep, block)
                extend(prv.at[block], ppot[sweep, block])
                if sweep == SWEEPS - 1:
                    mean_block(prv.at[block], acc)
                else:
                    log_block()

            tpot[sweep] = result()
            for i in reversed(range(n)):
                tpot_copy(sweep, i).start()

    for sweep in range(SWEEPS):
        source_pass(sweep)
        target_pass(sweep)

    @pl.when(has_prev)
    def _():
        pull_ref[...] = points_ref[...] - acc[...] / l_ref[...]

    @pl.when(jnp.logical_not(has_prev))
    def _():
        pull_ref[...] = jnp.zeros_like(pull_ref)

    @pl.when(has_next)
    def _():
        reset()
        acc[...] = jnp.zeros_like(acc)

        @pl.loop(0, n)
        def _(i):
            block = crossed(me, i, n)
            await_npot(SWEEPS - 1, block)
            extend(nxt.at[block], npot[SWEEPS - 1, block])
            mean_block(nxt.at[block], acc)

        pull_ref[...] = pull_ref[...] + (points_ref[...] - acc[...] / l_ref[...])

    for i in range(low, n, low):
        own_copy(i, me, i).wait_send()
    if low > 1:
        for i in range(0, n, low):
            own_copy(1, crossed(me, i, n), i + 1).wait_send()

    @pl.when(has_prev)
    def _():
        for i in range(n):
            to_prev(i).wait_send()
            for sweep in range(SWEEPS):
                tpot_copy(sweep, i).wait_send()

    @pl.when(has_next)
    def _():
        for i in range(n):
            to_next(i).wait_send()
            for sweep in range(SWEEPS):
                spot_copy(sweep, i).wait_send()


def per_device(times, n, particles, noise):
    points = particles[0]
    dim, width = points.shape
    dma = pltpu.SemaphoreType.DMA
    row = (1, width)
    pull = pl.pallas_call(
        functools.partial(kernel, times, n),
        out_shape=jax.ShapeDtypeStruct((dim, width), jnp.float32),
        in_specs=[pl.BlockSpec(memory_space=pltpu.VMEM)],
        out_specs=pl.BlockSpec(memory_space=pltpu.VMEM),
        scratch_shapes=[
            pltpu.VMEM((n, dim, width), jnp.bfloat16),
            pltpu.VMEM((n, dim, width), jnp.bfloat16),
            pltpu.VMEM((n, dim, width), jnp.bfloat16),
            pltpu.VMEM((SWEEPS, n) + row, jnp.float32),
            pltpu.VMEM((SWEEPS, n) + row, jnp.float32),
            pltpu.VMEM((SWEEPS,) + row, jnp.float32),
            pltpu.VMEM((SWEEPS,) + row, jnp.float32),
            pltpu.VMEM((dim + EXTRA, width), jnp.bfloat16),
            pltpu.VMEM((dim + EXTRA, width), jnp.bfloat16),
            pltpu.VMEM(row, jnp.float32),
            pltpu.VMEM(row, jnp.float32),
            pltpu.VMEM((dim, width), jnp.float32),
            dma((n,)), dma((n,)), dma((n,)), dma((n,)), dma((n,)), dma((n,)),
            dma((SWEEPS, n)), dma((SWEEPS, n)), dma((SWEEPS, n)), dma((SWEEPS, n)),
        ],
        compiler_params=pltpu.CompilerParams(collective_id=0, has_side_effects=True),
    )(points)
    advanced = points - STEP * pull + math.sqrt(2.0 * STEP * TEMP) * noise[0]
    return advanced[None]


def solution(mesh):
    times, n = mesh.shape["tm"], mesh.shape["dom"]
    assert n & (n - 1) == 0
    spec = P("tm", None, "dom")
    return jax.shard_map(
        functools.partial(per_device, times, n), mesh=mesh, in_specs=(spec, spec), out_specs=spec, check_vma=False)
```

```python
import functools
import math

import jax
import jax.numpy as jnp
from jax import lax
from jax.experimental import pallas as pl
from jax.experimental.pallas import tpu as pltpu
from jax.sharding import PartitionSpec as P

SWEEPS = 2
EPS = 4.0
STEP = 0.5
TEMP = 0.05
MESH = pl.DeviceIdType.MESH
EXTRA = 16
PIECE = 64
CHUNK = 256
LAG = 2


def crossed(me, i, n):
    total = 0
    bit = 1
    while bit < n:
        mine, its = (me // bit) % 2, (i // bit) % 2
        total = total + bit * (mine + its - 2 * mine * its)
        bit *= 2
    return total


def kernel(
    times, n, points_ref, pull_ref,
    own, nxt, prv, npot, ppot, spot, tpot, xa, ya, yb, sa, sb, pw, m_ref, l_ref, acc,
    own_s, own_r, nxt_s, nxt_r, prv_s, prv_r, npot_s, npot_r, ppot_s, ppot_r,
):
    t = lax.axis_index("tm")
    me = lax.axis_index("dom")
    dim, width = points_ref.shape
    has_next = t < times - 1
    has_prev = t > 0
    low = 2 if n > 1 else 1
    log_count = EPS * math.log(n * width)

    points = points_ref[...]
    rounded = points.astype(jnp.bfloat16)
    own[me] = rounded
    xa[pl.ds(0, dim), :] = (rounded.astype(jnp.float32) * (1.0 / EPS)).astype(jnp.bfloat16)
    rows = lax.broadcasted_iota(jnp.int32, (EXTRA, width), 0)
    xa[pl.ds(dim, EXTRA), :] = jnp.where(rows < 3, 1.0 / EPS, 0.0).astype(jnp.bfloat16)

    barrier = pltpu.get_barrier_semaphore()
    same = [i for i in range(1, n) if i % low == 0 or i == 1]
    for i in same:
        pl.semaphore_signal(barrier, inc=1, device_id=(t, crossed(me, i, n)), device_id_type=MESH)

    @pl.when(has_next)
    def _():
        pl.semaphore_signal(barrier, inc=1, device_id=(t + 1, me), device_id_type=MESH)

    @pl.when(has_prev)
    def _():
        pl.semaphore_signal(barrier, inc=1, device_id=(t - 1, me), device_id_type=MESH)

    sides = has_next.astype(jnp.int32) + has_prev.astype(jnp.int32)
    pl.semaphore_wait(barrier, len(same) + sides)

    def own_copy(i, block, slot):
        return pltpu.make_async_remote_copy(
            src_ref=own.at[block], dst_ref=own.at[block], send_sem=own_s.at[slot], recv_sem=own_r.at[block],
            device_id=(t, crossed(me, i, n)), device_id_type=MESH)

    def to_prev(block):
        return pltpu.make_async_remote_copy(
            src_ref=own.at[block], dst_ref=nxt.at[block], send_sem=nxt_s.at[block], recv_sem=nxt_r.at[block],
            device_id=(t - 1, me), device_id_type=MESH)

    def to_next(block):
        return pltpu.make_async_remote_copy(
            src_ref=own.at[block], dst_ref=prv.at[block], send_sem=prv_s.at[block], recv_sem=prv_r.at[block],
            device_id=(t + 1, me), device_id_type=MESH)

    for i in range(low, n, low):
        own_copy(i, me, i).start()

    def pass_on(i):
        block = crossed(me, i, n)
        if i > 0:
            own_copy(i if i % low == 0 else 1, block, 0).wait_recv()
        if i % low == 0 and low > 1:
            own_copy(1, block, i + 1).start()

        @pl.when(has_prev)
        def _():
            to_prev(block).start()

        @pl.when(has_next)
        def _():
            to_next(block).start()

    order = [0]
    for i in range(low, n, low):
        order += [i, i - low + 1] if low > 1 else [i]
    if low > 1:
        order.append(n - 1)
    def extend(y_ref, block_ref, pot):
        y_ref[pl.ds(0, dim), :] = block_ref[...]
        high = pot.astype(jnp.bfloat16).astype(jnp.float32)
        rest = pot - high
        middle = rest.astype(jnp.bfloat16).astype(jnp.float32)
        least = rest - middle
        pieces = jnp.where(rows == 0, high, jnp.where(rows == 1, middle, jnp.where(rows == 2, least, 0.0)))
        y_ref[pl.ds(dim, EXTRA), :] = pieces.astype(jnp.bfloat16)

    def folded(values, join):
        parts = [values[r:r + 8] for r in range(0, values.shape[0], 8)]
        while len(parts) > 1:
            parts = [join(parts[k], parts[k + 1]) for k in range(0, len(parts) - 1, 2)] + (
                [parts[-1]] if len(parts) % 2 else [])
        return parts[0]

    def reset():
        m_ref[...] = jnp.full_like(m_ref, -jnp.inf)
        l_ref[...] = jnp.zeros_like(l_ref)

    def step(y_ref, new_scores, old_scores, old_block, mean):
        m_old = m_ref[...]
        highest, total = None, None
        if old_scores is not None:
            for start in range(0, width, PIECE):
                here = pl.ds(start, PIECE)
                weights = jnp.exp(old_scores[here, :] - m_old)
                part = folded(weights, jnp.add)
                total = part if total is None else total + part
                if mean:
                    pw[here, :] = weights.astype(jnp.bfloat16)
        if new_scores is not None:
            for start in range(0, width, CHUNK):
                here = pl.ds(start, CHUNK)
                scores = lax.dot_general(
                    y_ref[:, here], xa[...], (((0,), (0,)), ((), ())), preferred_element_type=jnp.float32)
                new_scores[here, :] = scores
                top = folded(scores, jnp.maximum)
                highest = top if highest is None else jnp.maximum(highest, top)
        if old_scores is not None:
            sums = l_ref[...] + jnp.sum(total, axis=0, keepdims=True)
            if mean:
                for start in range(0, width, CHUNK):
                    here = pl.ds(start, CHUNK)
                    acc[...] += lax.dot_general(
                        old_block[:, here], pw[here, :], (((1,), (0,)), ((), ())),
                        preferred_element_type=jnp.float32)
        else:
            sums = l_ref[...]
        if new_scores is not None:
            m_new = jnp.maximum(m_old, jnp.max(highest, axis=0, keepdims=True))
            scale = jnp.exp(m_old - m_new)
            m_ref[...] = m_new
            sums = sums * scale
            if mean and old_scores is not None:
                acc[...] = acc[...] * scale
        l_ref[...] = sums

    def sweep_over(prepare, slots, mean):
        def do(i, y_ref, new, old):
            prepare(y_ref, i)
            step(y_ref, new, old, slots.at[crossed(me, i - 1, n)], mean)

        prepare(ya, 0)
        step(ya, sa, None, None, mean)
        if n > 2:
            @pl.loop(0, n // 2 - 1)
            def _(h):
                do(2 * h + 1, yb, sb, sa)
                do(2 * h + 2, ya, sa, sb)
        do(n - 1, yb, sb, sa)
        step(None, None, sb, slots.at[crossed(me, n - 1, n)], mean)

    def result():
        return -EPS * (m_ref[...] + jnp.log(l_ref[...])) + log_count

    def spot_copy(sweep, i):
        return pltpu.make_async_remote_copy(
            src_ref=spot.at[sweep], dst_ref=ppot.at[sweep, me], send_sem=ppot_s.at[sweep, i],
            recv_sem=ppot_r.at[sweep, me], device_id=(t + 1, crossed(me, i, n)), device_id_type=MESH)

    def tpot_copy(sweep, i):
        return pltpu.make_async_remote_copy(
            src_ref=tpot.at[sweep], dst_ref=npot.at[sweep, me], send_sem=npot_s.at[sweep, i],
            recv_sem=npot_r.at[sweep, me], device_id=(t - 1, crossed(me, i, n)), device_id_type=MESH)

    def await_ppot(sweep, block):
        pltpu.make_async_remote_copy(
            src_ref=spot.at[sweep], dst_ref=ppot.at[sweep, block], send_sem=ppot_s.at[sweep, 0],
            recv_sem=ppot_r.at[sweep, block], device_id=(t - 1, block), device_id_type=MESH).wait_recv()

    def await_npot(sweep, block):
        pltpu.make_async_remote_copy(
            src_ref=tpot.at[sweep], dst_ref=npot.at[sweep, block], send_sem=npot_s.at[sweep, 0],
            recv_sem=npot_r.at[sweep, block], device_id=(t + 1, block), device_id_type=MESH).wait_recv()

    def landed(block, slots, sends, recvs):
        pltpu.make_async_remote_copy(
            src_ref=own.at[block], dst_ref=slots.at[block], send_sem=sends.at[block], recv_sem=recvs.at[block],
            device_id=(t, me), device_id_type=MESH).wait_recv()

    def send_source(sweep):
        spot[sweep] = result()
        for i in reversed(range(n)):
            spot_copy(sweep, i).start()

    def first_prepare(y_ref, i):
        block = crossed(me, i, n)
        landed(block, nxt, nxt_s, nxt_r)
        extend(y_ref, nxt.at[block], -0.5 * jnp.sum(
            jnp.square(nxt[block].astype(jnp.float32)), axis=0, keepdims=True))

    @pl.when(has_next)
    def _():
        reset()

    def first_step(k):
        @pl.when(has_next)
        def _():
            y_ref, new, old = (ya, sa, sb) if k % 2 == 0 else (yb, sb, sa)
            first_prepare(y_ref, order[k])
            step(y_ref, new, old if k > 0 else None, None, False)

    for k in range(n):
        pass_on(order[k])
        if k >= LAG:
            first_step(k - LAG)
    for k in range(max(0, n - LAG), n):
        first_step(k)

    @pl.when(has_next)
    def _():
        step(None, None, sb if n % 2 == 0 else sa, None, False)
        send_source(0)

    def source_pass(sweep):
        def prepare(y_ref, i):
            block = crossed(me, i, n)
            await_npot(sweep - 1, block)
            extend(y_ref, nxt.at[block], npot[sweep - 1, block])

        @pl.when(has_next)
        def _():
            reset()
            sweep_over(prepare, nxt, False)
            send_source(sweep)

    def target_pass(sweep):
        def prepare(y_ref, i):
            block = crossed(me, i, n)
            if sweep == 0:
                landed(block, prv, prv_s, prv_r)
            await_ppot(sweep, block)
            extend(y_ref, prv.at[block], ppot[sweep, block])

        @pl.when(has_prev)
        def _():
            reset()
            mean = sweep == SWEEPS - 1
            if mean:
                acc[...] = jnp.zeros_like(acc)
            sweep_over(prepare, prv, mean)
            tpot[sweep] = result()
            for i in reversed(range(n)):
                tpot_copy(sweep, i).start()

    for sweep in range(SWEEPS):
        if sweep > 0:
            source_pass(sweep)
        target_pass(sweep)

    @pl.when(has_prev)
    def _():
        pull_ref[...] = points_ref[...] - acc[...] / l_ref[...]

    @pl.when(jnp.logical_not(has_prev))
    def _():
        pull_ref[...] = jnp.zeros_like(pull_ref)

    @pl.when(has_next)
    def _():
        reset()
        acc[...] = jnp.zeros_like(acc)

        def prepare(y_ref, i):
            block = crossed(me, i, n)
            await_npot(SWEEPS - 1, block)
            extend(y_ref, nxt.at[block], npot[SWEEPS - 1, block])

        sweep_over(prepare, nxt, True)
        pull_ref[...] = pull_ref[...] + (points_ref[...] - acc[...] / l_ref[...])

    for i in range(low, n, low):
        own_copy(i, me, i).wait_send()
    if low > 1:
        for i in range(0, n, low):
            own_copy(1, crossed(me, i, n), i + 1).wait_send()

    @pl.when(has_prev)
    def _():
        for i in range(n):
            to_prev(i).wait_send()
            for sweep in range(SWEEPS):
                tpot_copy(sweep, i).wait_send()

    @pl.when(has_next)
    def _():
        for i in range(n):
            to_next(i).wait_send()
            for sweep in range(SWEEPS):
                spot_copy(sweep, i).wait_send()


def per_device(times, n, particles, noise):
    points = particles[0]
    dim, width = points.shape
    dma = pltpu.SemaphoreType.DMA
    row = (1, width)
    pull = pl.pallas_call(
        functools.partial(kernel, times, n),
        out_shape=jax.ShapeDtypeStruct((dim, width), jnp.float32),
        in_specs=[pl.BlockSpec(memory_space=pltpu.VMEM)],
        out_specs=pl.BlockSpec(memory_space=pltpu.VMEM),
        scratch_shapes=[
            pltpu.VMEM((n, dim, width), jnp.bfloat16),
            pltpu.VMEM((n, dim, width), jnp.bfloat16),
            pltpu.VMEM((n, dim, width), jnp.bfloat16),
            pltpu.VMEM((SWEEPS, n) + row, jnp.float32),
            pltpu.VMEM((SWEEPS, n) + row, jnp.float32),
            pltpu.VMEM((SWEEPS,) + row, jnp.float32),
            pltpu.VMEM((SWEEPS,) + row, jnp.float32),
            pltpu.VMEM((dim + EXTRA, width), jnp.bfloat16),
            pltpu.VMEM((dim + EXTRA, width), jnp.bfloat16),
            pltpu.VMEM((dim + EXTRA, width), jnp.bfloat16),
            pltpu.VMEM((width, width), jnp.float32),
            pltpu.VMEM((width, width), jnp.float32),
            pltpu.VMEM((width, width), jnp.bfloat16),
            pltpu.VMEM(row, jnp.float32),
            pltpu.VMEM(row, jnp.float32),
            pltpu.VMEM((dim, width), jnp.float32),
            dma((n,)), dma((n,)), dma((n,)), dma((n,)), dma((n,)), dma((n,)),
            dma((SWEEPS, n)), dma((SWEEPS, n)), dma((SWEEPS, n)), dma((SWEEPS, n)),
        ],
        compiler_params=pltpu.CompilerParams(collective_id=0, has_side_effects=True),
    )(points)
    advanced = points - STEP * pull + math.sqrt(2.0 * STEP * TEMP) * noise[0]
    return advanced[None]


def solution(mesh):
    times, n = mesh.shape["tm"], mesh.shape["dom"]
    assert n & (n - 1) == 0
    spec = P("tm", None, "dom")
    return jax.shard_map(
        functools.partial(per_device, times, n), mesh=mesh, in_specs=(spec, spec), out_specs=spec, check_vma=False)
```

```python
import functools
import math

import jax
import jax.numpy as jnp
from jax import lax
from jax.experimental import pallas as pl
from jax.experimental.pallas import tpu as pltpu
from jax.sharding import PartitionSpec as P

SWEEPS = 2
EPS = 4.0
STEP = 0.5
TEMP = 0.05
MESH = pl.DeviceIdType.MESH
EXTRA = 16
PIECE = 64
CHUNK = 512
LAG = 4


def crossed(me, i, n):
    total = 0
    bit = 1
    while bit < n:
        mine, its = (me // bit) % 2, (i // bit) % 2
        total = total + bit * (mine + its - 2 * mine * its)
        bit *= 2
    return total


def kernel(
    times, n, points_ref, noise_ref, out_ref,
    own, nxt, prv, npot, ppot, spot, tpot, xa, ya, yb, sa, sb, pw, m_ref, l_ref, acc,
    own_s, own_r, nxt_s, nxt_r, prv_s, prv_r, npot_s, npot_r, ppot_s, ppot_r,
):
    t = lax.axis_index("tm")
    me = lax.axis_index("dom")
    dim, width = points_ref.shape
    has_next = t < times - 1
    has_prev = t > 0
    low = 2 if n > 1 else 1
    log_count = EPS * math.log(n * width)

    points = points_ref[...]
    rounded = points.astype(jnp.bfloat16)
    own[me] = rounded
    xa[pl.ds(0, dim), :] = (rounded.astype(jnp.float32) * (1.0 / EPS)).astype(jnp.bfloat16)
    rows = lax.broadcasted_iota(jnp.int32, (EXTRA, width), 0)
    xa[pl.ds(dim, EXTRA), :] = jnp.where(rows < 3, 1.0 / EPS, 0.0).astype(jnp.bfloat16)

    barrier = pltpu.get_barrier_semaphore()
    same = [i for i in range(1, n) if i % low == 0 or i == 1]
    for i in same:
        pl.semaphore_signal(barrier, inc=1, device_id=(t, crossed(me, i, n)), device_id_type=MESH)

    @pl.when(has_next)
    def _():
        pl.semaphore_signal(barrier, inc=1, device_id=(t + 1, me), device_id_type=MESH)

    @pl.when(has_prev)
    def _():
        pl.semaphore_signal(barrier, inc=1, device_id=(t - 1, me), device_id_type=MESH)

    sides = has_next.astype(jnp.int32) + has_prev.astype(jnp.int32)
    pl.semaphore_wait(barrier, len(same) + sides)

    def own_copy(i, block, slot):
        return pltpu.make_async_remote_copy(
            src_ref=own.at[block], dst_ref=own.at[block], send_sem=own_s.at[slot], recv_sem=own_r.at[block],
            device_id=(t, crossed(me, i, n)), device_id_type=MESH)

    def to_prev(block):
        return pltpu.make_async_remote_copy(
            src_ref=own.at[block], dst_ref=nxt.at[block], send_sem=nxt_s.at[block], recv_sem=nxt_r.at[block],
            device_id=(t - 1, me), device_id_type=MESH)

    def to_next(block):
        return pltpu.make_async_remote_copy(
            src_ref=own.at[block], dst_ref=prv.at[block], send_sem=prv_s.at[block], recv_sem=prv_r.at[block],
            device_id=(t + 1, me), device_id_type=MESH)

    for i in range(low, n, low):
        own_copy(i, me, i).start()

    def pass_on(i):
        block = crossed(me, i, n)
        if i > 0:
            own_copy(i if i % low == 0 else 1, block, 0).wait_recv()
        if i % low == 0 and low > 1:
            own_copy(1, block, i + 1).start()

        @pl.when(has_prev)
        def _():
            to_prev(block).start()

        @pl.when(has_next)
        def _():
            to_next(block).start()

    order = [0]
    for i in range(low, n, low):
        order += [i, i - low + 1] if low > 1 else [i]
    if low > 1:
        order.append(n - 1)
    def extend(y_ref, block_ref, pot):
        y_ref[pl.ds(0, dim), :] = block_ref[...]
        high = pot.astype(jnp.bfloat16).astype(jnp.float32)
        rest = pot - high
        middle = rest.astype(jnp.bfloat16).astype(jnp.float32)
        least = rest - middle
        pieces = jnp.where(rows == 0, high, jnp.where(rows == 1, middle, jnp.where(rows == 2, least, 0.0)))
        y_ref[pl.ds(dim, EXTRA), :] = pieces.astype(jnp.bfloat16)

    def folded(values, join):
        parts = [values[r:r + 8] for r in range(0, values.shape[0], 8)]
        while len(parts) > 1:
            parts = [join(parts[k], parts[k + 1]) for k in range(0, len(parts) - 1, 2)] + (
                [parts[-1]] if len(parts) % 2 else [])
        return parts[0]

    def reset():
        m_ref[...] = jnp.full_like(m_ref, -jnp.inf)
        l_ref[...] = jnp.zeros_like(l_ref)

    def step(y_ref, new_scores, old_scores, old_block, mean):
        m_old = m_ref[...]
        highest, total = None, None
        if old_scores is not None:
            for start in range(0, width, PIECE):
                here = pl.ds(start, PIECE)
                weights = jnp.exp(old_scores[here, :] - m_old)
                part = folded(weights, jnp.add)
                total = part if total is None else total + part
                if mean:
                    pw[here, :] = weights.astype(jnp.bfloat16)
        if new_scores is not None:
            for start in range(0, width, CHUNK):
                here = pl.ds(start, CHUNK)
                scores = lax.dot_general(
                    y_ref[:, here], xa[...], (((0,), (0,)), ((), ())), preferred_element_type=jnp.float32)
                new_scores[here, :] = scores
                top = folded(scores, jnp.maximum)
                highest = top if highest is None else jnp.maximum(highest, top)
        if old_scores is not None:
            sums = l_ref[...] + jnp.sum(total, axis=0, keepdims=True)
            if mean:
                for start in range(0, width, CHUNK):
                    here = pl.ds(start, CHUNK)
                    acc[...] += lax.dot_general(
                        old_block[:, here], pw[here, :], (((1,), (0,)), ((), ())),
                        preferred_element_type=jnp.float32)
        else:
            sums = l_ref[...]
        if new_scores is not None:
            m_new = jnp.maximum(m_old, jnp.max(highest, axis=0, keepdims=True))
            scale = jnp.exp(m_old - m_new)
            m_ref[...] = m_new
            sums = sums * scale
            if mean and old_scores is not None:
                acc[...] = acc[...] * scale
        l_ref[...] = sums

    def sweep_over(prepare, slots, mean):
        def do(i, y_ref, new, old):
            prepare(y_ref, i)
            step(y_ref, new, old, slots.at[crossed(me, i - 1, n)], mean)

        prepare(ya, 0)
        step(ya, sa, None, None, mean)
        if n > 2:
            @pl.loop(0, n // 2 - 1)
            def _(h):
                do(2 * h + 1, yb, sb, sa)
                do(2 * h + 2, ya, sa, sb)
        do(n - 1, yb, sb, sa)
        step(None, None, sb, slots.at[crossed(me, n - 1, n)], mean)

    def result():
        return -EPS * (m_ref[...] + jnp.log(l_ref[...])) + log_count

    def spot_copy(sweep, i):
        return pltpu.make_async_remote_copy(
            src_ref=spot.at[sweep], dst_ref=ppot.at[sweep, me], send_sem=ppot_s.at[sweep, i],
            recv_sem=ppot_r.at[sweep, me], device_id=(t + 1, crossed(me, i, n)), device_id_type=MESH)

    def tpot_copy(sweep, i):
        return pltpu.make_async_remote_copy(
            src_ref=tpot.at[sweep], dst_ref=npot.at[sweep, me], send_sem=npot_s.at[sweep, i],
            recv_sem=npot_r.at[sweep, me], device_id=(t - 1, crossed(me, i, n)), device_id_type=MESH)

    def await_ppot(sweep, block):
        pltpu.make_async_remote_copy(
            src_ref=spot.at[sweep], dst_ref=ppot.at[sweep, block], send_sem=ppot_s.at[sweep, 0],
            recv_sem=ppot_r.at[sweep, block], device_id=(t - 1, block), device_id_type=MESH).wait_recv()

    def await_npot(sweep, block):
        pltpu.make_async_remote_copy(
            src_ref=tpot.at[sweep], dst_ref=npot.at[sweep, block], send_sem=npot_s.at[sweep, 0],
            recv_sem=npot_r.at[sweep, block], device_id=(t + 1, block), device_id_type=MESH).wait_recv()

    def landed(block, slots, sends, recvs):
        pltpu.make_async_remote_copy(
            src_ref=own.at[block], dst_ref=slots.at[block], send_sem=sends.at[block], recv_sem=recvs.at[block],
            device_id=(t, me), device_id_type=MESH).wait_recv()

    def send_source(sweep):
        spot[sweep] = result()
        for i in reversed(range(n)):
            spot_copy(sweep, i).start()

    def first_prepare(y_ref, i):
        block = crossed(me, i, n)
        landed(block, nxt, nxt_s, nxt_r)
        extend(y_ref, nxt.at[block], -0.5 * jnp.sum(
            jnp.square(nxt[block].astype(jnp.float32)), axis=0, keepdims=True))

    @pl.when(has_next)
    def _():
        reset()

    def first_step(k):
        @pl.when(has_next)
        def _():
            y_ref, new, old = (ya, sa, sb) if k % 2 == 0 else (yb, sb, sa)
            first_prepare(y_ref, order[k])
            step(y_ref, new, old if k > 0 else None, None, False)

    for k in range(n):
        pass_on(order[k])
        if k >= LAG:
            first_step(k - LAG)
    for k in range(max(0, n - LAG), n):
        first_step(k)

    @pl.when(has_next)
    def _():
        step(None, None, sb if n % 2 == 0 else sa, None, False)
        send_source(0)

    def source_pass(sweep):
        def prepare(y_ref, i):
            block = crossed(me, i, n)
            await_npot(sweep - 1, block)
            extend(y_ref, nxt.at[block], npot[sweep - 1, block])

        @pl.when(has_next)
        def _():
            reset()
            sweep_over(prepare, nxt, False)
            send_source(sweep)

    def target_pass(sweep):
        def prepare(y_ref, i):
            block = crossed(me, i, n)
            if sweep == 0:
                landed(block, prv, prv_s, prv_r)
            await_ppot(sweep, block)
            extend(y_ref, prv.at[block], ppot[sweep, block])

        @pl.when(has_prev)
        def _():
            reset()
            mean = sweep == SWEEPS - 1
            if mean:
                acc[...] = jnp.zeros_like(acc)
            sweep_over(prepare, prv, mean)
            tpot[sweep] = result()
            for i in reversed(range(n)):
                tpot_copy(sweep, i).start()

    for sweep in range(SWEEPS):
        if sweep > 0:
            source_pass(sweep)
        target_pass(sweep)

    @pl.when(has_prev)
    def _():
        out_ref[...] = points_ref[...] - STEP * (points_ref[...] - acc[...] / l_ref[...]) + (
            math.sqrt(2.0 * STEP * TEMP) * noise_ref[...])

    @pl.when(jnp.logical_not(has_prev))
    def _():
        out_ref[...] = points_ref[...] + math.sqrt(2.0 * STEP * TEMP) * noise_ref[...]

    @pl.when(has_next)
    def _():
        reset()
        acc[...] = jnp.zeros_like(acc)

        def prepare(y_ref, i):
            block = crossed(me, i, n)
            await_npot(SWEEPS - 1, block)
            extend(y_ref, nxt.at[block], npot[SWEEPS - 1, block])

        sweep_over(prepare, nxt, True)
        out_ref[...] = out_ref[...] - STEP * (points_ref[...] - acc[...] / l_ref[...])

    for i in range(low, n, low):
        own_copy(i, me, i).wait_send()
    if low > 1:
        for i in range(0, n, low):
            own_copy(1, crossed(me, i, n), i + 1).wait_send()

    @pl.when(has_prev)
    def _():
        for i in range(n):
            to_prev(i).wait_send()
            for sweep in range(SWEEPS):
                tpot_copy(sweep, i).wait_send()

    @pl.when(has_next)
    def _():
        for i in range(n):
            to_next(i).wait_send()
            for sweep in range(SWEEPS):
                spot_copy(sweep, i).wait_send()


def per_device(times, n, particles, noise):
    points = particles[0]
    dim, width = points.shape
    dma = pltpu.SemaphoreType.DMA
    row = (1, width)
    advanced = pl.pallas_call(
        functools.partial(kernel, times, n),
        out_shape=jax.ShapeDtypeStruct((dim, width), jnp.float32),
        in_specs=[pl.BlockSpec(memory_space=pltpu.VMEM)] * 2,
        out_specs=pl.BlockSpec(memory_space=pltpu.VMEM),
        scratch_shapes=[
            pltpu.VMEM((n, dim, width), jnp.bfloat16),
            pltpu.VMEM((n, dim, width), jnp.bfloat16),
            pltpu.VMEM((n, dim, width), jnp.bfloat16),
            pltpu.VMEM((SWEEPS, n) + row, jnp.float32),
            pltpu.VMEM((SWEEPS, n) + row, jnp.float32),
            pltpu.VMEM((SWEEPS,) + row, jnp.float32),
            pltpu.VMEM((SWEEPS,) + row, jnp.float32),
            pltpu.VMEM((dim + EXTRA, width), jnp.bfloat16),
            pltpu.VMEM((dim + EXTRA, width), jnp.bfloat16),
            pltpu.VMEM((dim + EXTRA, width), jnp.bfloat16),
            pltpu.VMEM((width, width), jnp.float32),
            pltpu.VMEM((width, width), jnp.float32),
            pltpu.VMEM((width, width), jnp.bfloat16),
            pltpu.VMEM(row, jnp.float32),
            pltpu.VMEM(row, jnp.float32),
            pltpu.VMEM((dim, width), jnp.float32),
            dma((n,)), dma((n,)), dma((n,)), dma((n,)), dma((n,)), dma((n,)),
            dma((SWEEPS, n)), dma((SWEEPS, n)), dma((SWEEPS, n)), dma((SWEEPS, n)),
        ],
        compiler_params=pltpu.CompilerParams(collective_id=0, has_side_effects=True),
    )(points, noise[0])
    return advanced[None]


def solution(mesh):
    times, n = mesh.shape["tm"], mesh.shape["dom"]
    assert n & (n - 1) == 0
    spec = P("tm", None, "dom")
    return jax.shard_map(
        functools.partial(per_device, times, n), mesh=mesh, in_specs=(spec, spec), out_specs=spec, check_vma=False)
```
